256 devices in a mesh: row: 32 (over x, y, core), col: 8 (over z).
Axes of the slice: x: 4, y: 4, z: 8, core: 2. Of those that a mesh axis runs over, the one named last changes fastest.
Arguments:
- a_matrix: float32 [2048, 2048], P('row', 'col'), may hold values from -0.9 to 0.9
- b_matrix: float32 [2048, 2048], P('row', 'col'), may hold values from -0.9 to 0.9
- a_panel: float32 [2048, 1024], P('row', 'col'), may hold values from -0.9 to 0.9
- b_panel: float32 [2048, 1024], P('row', 'col'), may hold values from -0.9 to 0.9
Outputs:
- triangle: float32 [1024, 1024], P('row', 'col')
- pencil_cross: float32 [2048, 2048], P('row', 'col')
The draws below stay inside these ranges and needn't reach their ends.
All inputs are finite; a program needn't handle non-finite values.
Results may differ from the reference program's by a relative error of at most 0.0003.
Values sent between devices are 32-bit elements; how exact they have to be, the bound alone decides.
A program may use at most 64 MiB of HBM per device.

```python
import jax
import jax.numpy as jnp
from jax import lax

N = 2048
K = 1024


def block_scale(rng, dims, cuts, low, high):
    loudness = 1.0
    for position, parts in cuts:
        heights = jax.random.uniform(jax.random.fold_in(jax.random.fold_in(rng, 6), position), (parts,), jnp.float32, low / len(cuts), high / len(cuts))
        loudness = loudness * jnp.repeat(jnp.exp(heights), dims[position] // parts).reshape((-1,) + (1,) * (len(dims) - 1 - position))
    return loudness


def scatter_about(key, shape, deviation, most, cuts=(), held_as=jnp.bfloat16):
    array = deviation * jax.random.normal(key, shape, jnp.float32)
    if cuts:
        array = array * block_scale(key, shape, cuts, -0.22, 0.18)
    return jnp.clip(array, -most, most).astype(held_as)


def setup_inputs(seed: int = 0) -> dict:
    splits = jax.random.split(jax.random.key(seed), 5)
    a_matrix = scatter_about(splits[0], (N, N), 0.15, 0.9, ((0, 32), (1, 8)), jnp.float32)
    b_matrix = scatter_about(splits[1], (N, N), 0.15, 0.9, ((0, 32), (1, 8)), jnp.float32)
    a_panel = scatter_about(splits[2], (N, K), 0.15, 0.9, ((0, 32), (1, 8)), jnp.float32)
    b_panel = scatter_about(splits[3], (N, K), 0.15, 0.9, ((0, 32), (1, 8)), jnp.float32)
    return {"a_matrix": a_matrix, "b_matrix": b_matrix, "a_panel": a_panel, "b_panel": b_panel}


HIGHEST = lax.Precision.HIGHEST

def reference(a_matrix, b_matrix, a_panel, b_panel):
    stacked = jnp.concatenate([b_panel, -a_panel], 0)
    q_full, r_full = jnp.linalg.qr(stacked)
    diag_signs = jnp.sign(jnp.diagonal(r_full))
    triangle = r_full * diag_signs[:, None]
    q_full = q_full * diag_signs[None, :]
    upper_rows = q_full[:N]
    lower_rows = q_full[N:]
    z_block = jnp.dot(lower_rows.T, b_matrix, precision=HIGHEST)
    v_block = jnp.dot(upper_rows, z_block, precision=HIGHEST)
    pencil_cross = -jnp.dot(a_matrix.T, v_block, precision=HIGHEST)
    return (triangle, pencil_cross)
```

```python
import jax
import jax.numpy as jnp
from jax import lax
from jax.experimental import pallas as pl
from jax.experimental.pallas import tpu as pltpu
from jax.sharding import PartitionSpec as P

HIGHEST = lax.Precision.HIGHEST
MESH = pl.DeviceIdType.MESH
B = 128
ROWS = 32
COLS = 8
CHIPS = 16
K = COLS * B
CD_STEP = 3


def dot_t(a, b):
    return lax.dot_general(
        a, b, (((0,), (0,)), ((), ())), precision=HIGHEST, preferred_element_type=jnp.float32
    )


def dot(a, b):
    return jnp.dot(a, b, precision=HIGHEST, preferred_element_type=jnp.float32)


def lane(x, k):
    return jnp.broadcast_to(x[:, k : k + 1], x.shape)


def sub(x, k):
    return jnp.broadcast_to(x[k : k + 1, :], x.shape)


def factor_block(d_ref, r_ref, li_ref):
    srow = lax.broadcasted_iota(jnp.int32, (8, B), 0)
    lcol = lax.broadcasted_iota(jnp.int32, (8, B), 1)
    groups = B // 8
    left = [d_ref[8 * g : 8 * g + 8, :] for g in range(groups)]
    right = [jnp.where(lcol == srow + 8 * g, 1.0, 0.0).astype(jnp.float32) for g in range(groups)]
    for i in range(groups):
        p, q = left[i], right[i]
        cols = [lane(p, 8 * i + m) for m in range(8)]
        rp = jnp.zeros((8, B), jnp.float32)
        rq = rp
        for m in range(8):
            pivot = sub(cols[m], m)
            inv = 1.0 / pivot
            root = lax.rsqrt(pivot)
            f = jnp.where(srow == m, 1.0 - inv, cols[m] * inv)
            pm, qm = sub(p, m), sub(q, m)
            rp = jnp.where(srow == m, pm * root, rp)
            rq = jnp.where(srow == m, qm * root, rq)
            p = p - f * pm
            q = q - f * qm
            for n in range(m + 1, 8):
                cols[n] = cols[n] - f * sub(cols[n], m)
        r_ref[8 * i : 8 * i + 8, :] = jnp.where(lcol >= srow + 8 * i, rp, 0.0)
        li_ref[8 * i : 8 * i + 8, :] = rq
        yp = [sub(p, m) for m in range(8)]
        yq = [sub(q, m) for m in range(8)]
        for g in range(i + 1, groups):
            c = [lane(left[g], 8 * i + m) for m in range(8)]
            u, v = left[g], right[g]
            for m in range(8):
                u = u - c[m] * yp[m]
                v = v - c[m] * yq[m]
            left[g], right[g] = u, v


def kernel(
    am, bm, ap, bp, tri, out,
    zb, pg, rg, sg, gw, pd, pcx, rd, rc, sd, sc, rhs, rr, lis, dd, dr, oo,
    z_s, z_r, g_s, g_r, y_s, y_r, a_s, a_r, p_s, p_r, d_s, d_r, c_s, c_r, e_s, e_r, f_s, f_r,
):
    k = lax.axis_index("row")
    n = lax.axis_index("col")
    t = k // 2
    core = lax.rem(k, 2)

    barrier = pltpu.get_barrier_semaphore()
    for s in range(1, COLS):
        pl.semaphore_signal(barrier, inc=1, device_id=(k, lax.rem(n + s, COLS)), device_id_type=MESH)
    for s in range(1, ROWS):
        pl.semaphore_signal(barrier, inc=1, device_id=(lax.rem(k + s, ROWS), n), device_id_type=MESH)
    pl.semaphore_wait(barrier, COLS - 1 + ROWS - 1)

    def send(src, dst, ssem, rsem, row, col):
        pltpu.make_async_remote_copy(
            src_ref=src, dst_ref=dst, send_sem=ssem, recv_sem=rsem, device_id=(row, col), device_id_type=MESH
        ).start()

    def local(src, dst, sem):
        pltpu.make_async_copy(src, dst, sem).start()

    def take(ref, sem):
        pltpu.make_async_copy(ref, ref, sem).wait()

    for s in (1, 7, 2, 6, 3, 5, 4):
        to = lax.rem(n + s, COLS)
        send(bp, zb.at[n, 0:64], z_s, z_r.at[n], k, to)
        send(ap, zb.at[n, 64:128], z_s, z_r.at[n], k, to)
    local(bp, zb.at[n, 0:64], z_r.at[n])
    local(ap, zb.at[n, 64:128], z_r.at[n])

    def near(s):
        return lax.rem(n + s + COLS, COLS)

    for s in (0, 1, -1, 2, -2):
        take(zb.at[near(s)], z_r.at[near(s)])

    lows, highs, mine = [], [], []
    for d in range(5):
        i, j = near(-(d // 2)), near((d + 1) // 2)
        lo, hi = jnp.minimum(i, j), jnp.maximum(i, j)
        lows.append(lo)
        highs.append(hi)
        mine.append(lax.rem(lo, 2) == core)
    for d in range(5):
        def share(d=d):
            pg[d] = dot_t(zb[lows[d]], zb[highs[d]])
            to_core = lax.rem(lows[d], 2)
            for s in range(1, CHIPS):
                to = lax.rem(t + s, CHIPS)
                send(pg.at[d, pl.ds(pl.multiple_of(8 * to, 8), 8)], rg.at[d, k], g_s.at[d], g_r.at[d], 2 * to + to_core, n)
            own = pg.at[d, pl.ds(pl.multiple_of(8 * t, 8), 8)]

            @pl.when(mine[d])
            def _():
                local(own, rg.at[d, k], g_r.at[d])

            @pl.when(jnp.logical_not(mine[d]))
            def _():
                send(own, rg.at[d, k], g_s.at[d], g_r.at[d], 2 * t + 1 - core, n)

        if d < 4:
            share()
        else:
            pl.when(n < 4)(share)

    for s in (3, -3, 4):
        take(zb.at[near(s)], z_r.at[near(s)])
    for c in range(COLS):
        pd[c * B : (c + 1) * B, :] = dot_t(zb[c, 64:128, :], bm[...])
        pcx[c * B : (c + 1) * B, :] = dot_t(zb[c, 0:64, :], am[...])

    for d in range(5):
        use = mine[d] if d < 4 else jnp.logical_and(mine[d], n < 4)

        @pl.when(use)
        def _(d=d):
            take(rg.at[d], g_r.at[d])
            sg[d] = jnp.sum(rg[d], axis=0)
            row = pl.ds(pl.multiple_of(lows[d] * B + 8 * t, 8), 8)
            col = pl.ds(pl.multiple_of(highs[d] * B, B), B)
            local(sg.at[d], gw.at[row, col], y_r.at[lows[d]])
            for s in (1, 7, 2, 6, 3, 5, 4):
                send(sg.at[d], gw.at[row, col], y_s.at[d], y_r.at[lows[d]], k, lax.rem(n + s, COLS))

    for a in range(COLS):
        @pl.when(core == a % 2)
        def _(a=a):
            piece = gw.at[pl.ds(pl.multiple_of(a * B + 8 * t, 8), 8), a * B : K]
            take(piece, y_r.at[a])
            for s in range(1, CHIPS):
                send(piece, piece, a_s.at[a], a_r.at[a], 2 * lax.rem(t + s, CHIPS) + core, n)

    for s in range(1, ROWS):
        to = lax.rem(k + s, ROWS)
        rows = pl.ds(pl.multiple_of(32 * to, 32), 32)
        send(pd.at[rows], rd.at[k], d_s, d_r, to, n)
        send(pcx.at[rows], rc.at[k], c_s, c_r, to, n)
    own_rows = pl.ds(pl.multiple_of(32 * k, 32), 32)
    local(pd.at[own_rows], rd.at[k], d_r)
    local(pcx.at[own_rows], rc.at[k], c_r)

    def hand_over(a):
        @pl.when(core == a % 2)
        def _():
            take(gw.at[a * B : a * B + 120, a * B : K], a_r.at[a])
            panel = gw.at[a * B : (a + 1) * B, a * B : K]
            send(panel, panel, p_s.at[a], p_r.at[a], k + 1 - 2 * core, n)

    def arrived(a):
        @pl.when(core != a % 2)
        def _():
            take(gw.at[a * B : (a + 1) * B, a * B : K], p_r.at[a])

    def spread_products():
        take(rd, d_r)
        take(rc, c_r)
        sd[...] = jnp.sum(rd[...], axis=0)
        sc[...] = jnp.sum(rc[...], axis=0)
        for s in range(1, ROWS):
            send(sd, rhs.at[own_rows, B : 3 * B], e_s, e_r, lax.rem(k + s, ROWS), n)
        local(sd, rhs.at[own_rows, B : 3 * B], e_r)
        for h in range(2):
            for o in range(2):
                r_to = 4 * n + 2 * h + o
                piece = sc.at[:, h * B : (h + 1) * B]
                there = rhs.at[own_rows, 0:B]
                for s in range(1, COLS):
                    send(piece, there, f_s, f_r, r_to, lax.rem(n + s, COLS))

                @pl.when(r_to == k)
                def _():
                    local(piece, there, f_r)

                @pl.when(r_to != k)
                def _():
                    send(piece, there, f_s, f_r, r_to, n)

    hand_over(0)
    hand_over(1)

    @pl.loop(0, COLS)
    def _(p):
        for a in range(COLS):
            @pl.when(p == a)
            def _(a=a):
                if a + 2 < COLS:
                    hand_over(a + 2)
                if a == CD_STEP:
                    spread_products()
                arrived(a)
                r0, r1 = a * B, (a + 1) * B
                if a:
                    s = gw[r0:r1, r0:K] - dot_t(rr[0:r0, r0:r1], rr[0:r0, r0:K])
                    dd[...] = s[:, 0:B]
                    if a + 1 < COLS:
                        rr[r0:r1, r1:K] = s[:, B:]
                else:
                    dd[...] = gw[r0:r1, r0:r1]
                    rr[r0:r1, r1:K] = gw[r0:r1, r1:K]
        factor_block(dd, dr, lis.at[p])
        for a in range(COLS):
            @pl.when(p == a)
            def _(a=a):
                r0, r1 = a * B, (a + 1) * B
                rr[r0:r1, r0:r1] = dr[...]
                if a + 1 < COLS:
                    rr[r0:r1, r1:K] = dot(lis[a], rr[r0:r1, r1:K])

    mine_r = k // 4

    @pl.when(n >= mine_r)
    def _():
        tri[...] = rr[own_rows, pl.ds(pl.multiple_of(n * B, B), B)]

    @pl.when(n < mine_r)
    def _():
        tri[...] = jnp.zeros_like(tri)

    take(rhs.at[:, B : 3 * B], e_r)
    take(rhs.at[:, 0:B], f_r)
    for a in range(COLS):
        r0, r1 = a * B, (a + 1) * B
        s = rhs[r0:r1, :]
        x = dot(lis[a], s)
        rhs[r0:r1, :] = x
        if a + 1 < COLS:
            rhs[r1:K, :] -= dot_t(rr[r0:r1, r1:K], x)
    oo[...] = dot_t(rhs[:, 0:B], rhs[:, B : 3 * B])
    out[...] = oo[pl.ds(pl.multiple_of(64 * core, 64), 64), :]

    take(zb.at[0:7], z_s)
    for d in range(5):
        def left_share(d=d):
            @pl.when(mine[d])
            def _():
                take(rg.at[d, 0:15], g_s.at[d])
                take(rg.at[d, 0:7], y_s.at[d])

            @pl.when(jnp.logical_not(mine[d]))
            def _():
                take(rg.at[d, 0:16], g_s.at[d])

        if d < 4:
            left_share()
        else:
            pl.when(n < 4)(left_share)
    for a in range(COLS):
        @pl.when(core == a % 2)
        def _(a=a):
            take(gw.at[a * B : a * B + 120, a * B : K], a_s.at[a])
            take(gw.at[a * B : (a + 1) * B, a * B : K], p_s.at[a])
    take(rd.at[0:31], d_s)
    take(rc.at[0:31], c_s)
    take(rd.at[0:31], e_s)

    @pl.when(k // 4 == n)
    def _():
        take(rhs.at[0 : K - 32, 0:B], f_s)

    @pl.when(k // 4 != n)
    def _():
        take(rhs.at[:, 0:B], f_s)


def local_step(am, bm, ap, bp):
    f32 = jnp.float32
    vmem = pltpu.VMEM
    dma = pltpu.SemaphoreType.DMA
    return pl.pallas_call(
        kernel,
        out_shape=(jax.ShapeDtypeStruct((32, B), f32), jax.ShapeDtypeStruct((64, 256), f32)),
        in_specs=[pl.BlockSpec(memory_space=vmem)] * 4,
        out_specs=[pl.BlockSpec(memory_space=vmem)] * 2,
        scratch_shapes=[
            vmem((COLS, B, B), f32),
            vmem((5, B, B), f32),
            vmem((5, ROWS, 8, B), f32),
            vmem((5, 8, B), f32),
            vmem((K, K), f32),
            vmem((K, 256), f32),
            vmem((K, 256), f32),
            vmem((ROWS, 32, 256), f32),
            vmem((ROWS, 32, 256), f32),
            vmem((32, 256), f32),
            vmem((32, 256), f32),
            vmem((K, 3 * B), f32),
            vmem((K, K), f32),
            vmem((COLS, B, B), f32),
            vmem((B, B), f32),
            vmem((B, B), f32),
            vmem((B, 256), f32),
            dma, dma((COLS,)),
            dma((5,)), dma((5,)),
            dma((5,)), dma((COLS,)),
            dma((COLS,)), dma((COLS,)),
            dma((COLS,)), dma((COLS,)),
            dma, dma, dma, dma, dma, dma, dma, dma,
        ],
        compiler_params=pltpu.CompilerParams(
            collective_id=0, has_side_effects=True, vmem_limit_bytes=60 * 2**20
        ),
    )(am, bm, ap, bp)


def solution(mesh):
    spec = P("row", "col")
    return jax.shard_map(
        local_step, mesh=mesh, in_specs=(spec,) * 4, out_specs=(spec, spec), check_vma=False
    )
```

```python
import jax
import jax.numpy as jnp
from jax import lax
from jax.experimental import pallas as pl
from jax.experimental.pallas import tpu as pltpu
from jax.sharding import PartitionSpec as P

HIGHEST = lax.Precision.HIGHEST
MESH = pl.DeviceIdType.MESH
B = 128
ROWS = 32
COLS = 8
CHIPS = 16
K = COLS * B
PAIR_C_STEP = 1
PAIR_D_STEP = 3
SUM_C_STEP = 4
SUM_D_STEP = 5
SPREAD_STEP = 5
HAND_D_STEP = 7


def dot_t(a, b):
    return lax.dot_general(
        a, b, (((0,), (0,)), ((), ())), precision=HIGHEST, preferred_element_type=jnp.float32
    )


def dot(a, b):
    return jnp.dot(a, b, precision=HIGHEST, preferred_element_type=jnp.float32)


def split(x):
    high = x.astype(jnp.bfloat16)
    return high, (x - high.astype(jnp.float32)).astype(jnp.bfloat16)


def dot_split(a, b, dims):
    (ah, al), (bh, bl) = split(a), split(b)

    def part(x, y):
        return lax.dot_general(x, y, (dims, ((), ())), preferred_element_type=jnp.float32)

    return part(ah, bh) + (part(ah, bl) + part(al, bh))


def fast_t(a, b):
    return dot_split(a, b, ((0,), (0,)))


def fast(a, b):
    return dot_split(a, b, ((1,), (0,)))


def lane(x, k):
    return jnp.broadcast_to(x[:, k : k + 1], x.shape)


def sub(x, k):
    return jnp.broadcast_to(x[k : k + 1, :], x.shape)


def total(terms):
    while len(terms) > 1:
        odd = terms[len(terms) - len(terms) % 2 :]
        terms = [terms[m] + terms[m + 1] for m in range(0, len(terms) - 1, 2)] + odd
    return terms[0]


def factor_block(d_ref, r_ref, li_ref):
    srow = lax.broadcasted_iota(jnp.int32, (8, B), 0)
    lcol = lax.broadcasted_iota(jnp.int32, (8, B), 1)
    groups = B // 8
    left = [d_ref[8 * g : 8 * g + 8, :] for g in range(groups)]
    right = [jnp.where(lcol == srow + 8 * g, 1.0, 0.0).astype(jnp.float32) for g in range(groups)]
    cols = [lane(left[0], m) for m in range(8)]
    for i in range(groups):
        p, q = left[i], right[i]
        more = i + 1 < groups
        ahead = []
        if more:
            by = [lane(left[i + 1], 8 * i + m) for m in range(8)]
            later = [lane(left[i + 1], 8 * i + 8 + m) for m in range(8)]
            ahead = [lane(p, 8 * i + 8 + m) for m in range(8)]
        rp = jnp.zeros((8, B), jnp.float32)
        rq = rp
        for m in range(8):
            pivot = sub(cols[m], m)
            inv = 1.0 / pivot
            root = lax.rsqrt(pivot)
            f = jnp.where(srow == m, 1.0 - inv, cols[m] * inv)
            for c in range(m + 1, 8):
                cols[c] = cols[c] - f * sub(cols[c], m)
            pm, qm = sub(p, m), sub(q, m)
            rp = jnp.where(srow == m, pm * root, rp)
            rq = jnp.where(srow == m, qm * root, rq)
            p = p - f * pm
            q = q - f * qm
            ahead = [x - f * sub(x, m) for x in ahead]
        r_ref[8 * i : 8 * i + 8, :] = jnp.where(lcol >= srow + 8 * i, rp, 0.0)
        li_ref[8 * i : 8 * i + 8, :] = rq
        yp = [sub(p, m) for m in range(8)]
        yq = [sub(q, m) for m in range(8)]
        if more:
            cols = [later[c] - total([by[m] * sub(ahead[c], m) for m in range(8)]) for c in range(8)]
        for g in range(i + 1, groups):
            w = by if g == i + 1 else [lane(left[g], 8 * i + m) for m in range(8)]
            left[g] = left[g] - total([w[m] * yp[m] for m in range(8)])
            right[g] = right[g] - total([w[m] * yq[m] for m in range(8)])


def place(b):
    return b // 2 + 4 * (b % 2)


def held(a, parity):
    first = a + 1 if (a + 1) % 2 == parity else a + 2
    return (first // 2 + 4 * parity) * B, (4 + 4 * parity) * B


def kernel(
    am, bm, ap, bp, tri, out,
    av, bv, tv, ov, zb, pg, rg, sg, gc, gd, gw, pd, pcx, qd, qc, rd, rc, sd, sc, cz, dl, rhs, rr, lis, dd, dr, oo,
    z_s, z_r, w_s, g_s, g_r, y_s, y_r, yd_r, b_s, b_r, a_s, a_r, p_s, p_r,
    q_s, q_r, d_s, d_r, c_s, c_r, e_s, e_r, h_s, h_r, f_s, f_r, i_s, i_r, o_r, m_r,
):
    k = lax.axis_index("row")
    n = lax.axis_index("col")
    t = k // 2
    core = lax.rem(k, 2)

    pltpu.make_async_copy(am, av, m_r.at[0]).start()
    pltpu.make_async_copy(bm, bv, m_r.at[1]).start()
    barrier = pltpu.get_barrier_semaphore()
    for s in range(1, COLS):
        pl.semaphore_signal(barrier, inc=1, device_id=(k, lax.rem(n + s, COLS)), device_id_type=MESH)
    for s in range(1, ROWS):
        pl.semaphore_signal(barrier, inc=1, device_id=(lax.rem(k + s, ROWS), n), device_id_type=MESH)
    pl.semaphore_wait(barrier, COLS - 1 + ROWS - 1)

    def send(src, dst, ssem, rsem, row, col):
        pltpu.make_async_remote_copy(
            src_ref=src, dst_ref=dst, send_sem=ssem, recv_sem=rsem, device_id=(row, col), device_id_type=MESH
        ).start()

    def local(src, dst, sem):
        pltpu.make_async_copy(src, dst, sem).start()

    def take(ref, sem):
        pltpu.make_async_copy(ref, ref, sem).wait()

    def near(s):
        return lax.rem(n + s + COLS, COLS)

    def send_panels(steps, sem):
        for s in steps:
            send(bp, zb.at[n, 0:64], sem, z_r.at[n], k, near(s))
            send(ap, zb.at[n, 64:128], sem, z_r.at[n], k, near(s))

    send_panels((1, -1, 2, -2), z_s)
    local(bp, zb.at[n, 0:64], z_r.at[n])
    local(ap, zb.at[n, 64:128], z_r.at[n])
    lows, highs, mine = [], [], []
    for d in range(5):
        i, j = near(-(d // 2)), near((d + 1) // 2)
        lo, hi = jnp.minimum(i, j), jnp.maximum(i, j)
        lows.append(lo)
        highs.append(hi)
        mine.append(lax.rem(hi, 2) == core)

    def where_needed(d, body):
        if d < 4:
            body()
        else:
            pl.when(n < 4)(body)

    def share(d):
        def body():
            pg[d] = dot_t(zb[lows[d]], zb[highs[d]])
            to_core = lax.rem(highs[d], 2)
            for s in range(1, CHIPS):
                to = lax.rem(t + s, CHIPS)
                send(pg.at[d, pl.ds(pl.multiple_of(8 * to, 8), 8)], rg.at[d, k], g_s.at[d], g_r.at[d], 2 * to + to_core, n)
            own = pg.at[d, pl.ds(pl.multiple_of(8 * t, 8), 8)]

            @pl.when(mine[d])
            def _():
                local(own, rg.at[d, k], g_r.at[d])

            @pl.when(jnp.logical_not(mine[d]))
            def _():
                send(own, rg.at[d, k], g_s.at[d], g_r.at[d], 2 * t + 1 - core, n)

        where_needed(d, body)

    def add_up(d):
        def body():
            @pl.when(mine[d])
            def _():
                take(rg.at[d], g_r.at[d])
                sg[d] = jnp.sum(rg[d], axis=0)
                if d == 0:
                    there, sem = gc.at[n], yd_r.at[n]
                else:
                    row = pl.ds(pl.multiple_of(lows[d] * B + 8 * t, 8), 8)
                    pos = highs[d] // 2 + 4 * core
                    there, sem = gw.at[row, pl.ds(pl.multiple_of(pos * B, B), B)], y_r.at[lows[d]]
                local(sg.at[d], there, sem)
                for s in (1, -1, 2, -2, 3, -3, 4):
                    send(sg.at[d], there, y_s.at[d], sem, k, near(s))

        where_needed(d, body)

    rows8 = pl.ds(pl.multiple_of(8 * t, 8), 8)

    def send_diagonal(a):
        @pl.when(core == a % 2)
        def _():
            take(gc.at[a], yd_r.at[a])
            for s in range(1, ROWS):
                send(gc.at[a], gd.at[a, rows8], b_s.at[a], b_r.at[a], lax.rem(k + s, ROWS), n)
            local(gc.at[a], gd.at[a, rows8], b_r.at[a])

    def send_rows(a):
        for parity in range(2):
            c0, c1 = held(a, parity)
            if c0 < c1:
                @pl.when(core == parity)
                def _(c0=c0, c1=c1):
                    piece = gw.at[pl.ds(pl.multiple_of(a * B + 8 * t, 8), 8), c0:c1]
                    take(piece, y_r.at[a])
                    for s in range(1, CHIPS):
                        sem = a_r.at[a] if a else o_r.at[s]
                        to = 2 * lax.rem(t + s, CHIPS)
                        send(piece, piece, a_s.at[a], sem, to + core, n)
                        if a == 1:
                            send(piece, piece, p_s.at[a], p_r.at[a], to + 1 - core, n)
                    if a < 2:
                        send(piece, piece, p_s.at[a], p_r.at[a], k + 1 - 2 * core, n)

    take(zb.at[n], z_r.at[n])
    share(0)
    take(zb.at[near(1)], z_r.at[near(1)])
    share(1)
    add_up(0)
    take(zb.at[near(-1)], z_r.at[near(-1)])
    share(2)
    take(zb.at[near(2)], z_r.at[near(2)])
    share(3)
    take(zb.at[near(-2)], z_r.at[near(-2)])
    share(4)
    send_panels((3, -3, 4), w_s)
    send_diagonal(0)
    for d in range(1, 5):
        add_up(d)

    def form_products():
        take(av, m_r.at[0])
        take(bv, m_r.at[1])
        for s in (3, -3, 4):
            take(zb.at[near(s)], z_r.at[near(s)])
        for c in range(COLS):
            d_part = fast_t(zb[c, 64:128, :], bv[...])
            c_part = fast_t(zb[c, 0:64, :], av[...])
            for e in range(4):
                r = 4 * c + e
                pd[r % 2, r // 2] = d_part[32 * e : 32 * e + 32, :]
                pcx[r % 2, r // 2] = c_part[32 * e : 32 * e + 32, :]
        send(pcx.at[1 - core], qc, q_s.at[1], q_r.at[1], k + 1 - 2 * core, n)
        send(pd.at[1 - core], qd, q_s.at[0], q_r.at[0], k + 1 - 2 * core, n)

    own_rows = pl.ds(pl.multiple_of(32 * k, 32), 32)

    def hand_over(a):
        for parity in range(2):
            c0, c1 = held(a, parity)
            if c0 < c1:
                @pl.when(core == parity)
                def _(c0=c0, c1=c1):
                    if a == 0:
                        for s in range(1, CHIPS):
                            source = lax.rem(t - s + CHIPS, CHIPS)
                            piece = gw.at[pl.ds(pl.multiple_of(8 * source, 8), 8), c0:c1]
                            take(piece, o_r.at[s])
                            send(piece, piece, p_s.at[a], p_r.at[a], k + 1 - 2 * core, n)
                    else:
                        take(gw.at[a * B : a * B + 120, c0:c1], a_r.at[a])
                    if a > 1:
                        panel = gw.at[a * B : (a + 1) * B, c0:c1]
                        send(panel, panel, p_s.at[a], p_r.at[a], k + 1 - 2 * core, n)

    def arrived(a):
        for parity in range(2):
            c0, c1 = held(a, parity)
            if c0 < c1:
                @pl.when(core != parity)
                def _(c0=c0, c1=c1):
                    take(gw.at[a * B : (a + 1) * B, c0:c1], p_r.at[a])

    def pair_up(index, got, ours, there, ssem, rsem):
        take(got, q_r.at[index])
        got[...] += ours[core]
        for s in range(1, CHIPS):
            to = lax.rem(t + s, CHIPS)
            send(got.at[to], there.at[t], ssem, rsem, 2 * to + core, n)
        local(got.at[t], there.at[t], rsem)

    def sum_c():
        take(rc, c_r)
        sc[...] = jnp.sum(rc[...], axis=0)
        for s in (1, -1, 2, -2, 3, -3, 4):
            send(sc, cz.at[n], h_s, h_r, k, near(s))
        local(sc, cz.at[n], h_r)

    def sum_d():
        take(rd, d_r)
        sd[...] = jnp.sum(rd[...], axis=0)
        for s in range(1, CHIPS):
            send(sd, dl.at[core, t], e_s, e_r, 2 * lax.rem(t + s, CHIPS) + core, n)
        local(sd, dl.at[core, t], e_r)

    def hand_d():
        take(dl.at[core], e_r)
        send(dl.at[core], dl.at[core], i_s, i_r, k + 1 - 2 * core, n)

    def spread_products():
        take(cz, h_r)
        for s in range(ROWS):
            to = lax.rem(k + s, ROWS)
            half = pl.ds(pl.multiple_of(lax.rem(to // 2, 2) * B, B), B)
            piece, there = cz.at[to // 4, :, half], rhs.at[own_rows, 0:B]
            if s:
                send(piece, there, f_s, f_r, to, n)
            else:
                local(piece, there, f_r)

    @pl.loop(0, COLS)
    def _(p):
        for a in range(COLS):
            @pl.when(p == a)
            def _(a=a):
                if a == PAIR_C_STEP:
                    pair_up(1, qc, pcx, rc, c_s, c_r)
                if a == PAIR_D_STEP:
                    pair_up(0, qd, pd, rd, d_s, d_r)
                if a == SUM_C_STEP:
                    sum_c()
                if a == SUM_D_STEP:
                    sum_d()
                if a == HAND_D_STEP:
                    hand_d()
                take(gd.at[a], b_r.at[a])
                r0, r1 = a * B, (a + 1) * B
                if a:
                    u = rr[0:r0, r0:r1]
                    dd[...] = gd[a] - dot_t(u, u)
                else:
                    dd[...] = gd[0]
        factor_block(dd, dr, lis.at[p])
        for a in range(COLS):
            @pl.when(p == a)
            def _(a=a):
                r0, r1 = a * B, (a + 1) * B
                if a == SPREAD_STEP:
                    spread_products()
                rr[r0:r1, r0:r1] = dr[...]
                if a + 1 < COLS:
                    if a == 0:
                        send_rows(0)
                        form_products()
                        send_diagonal(1)
                        send_rows(1)
                        hand_over(0)
                    if a == 1:
                        hand_over(1)
                    arrived(a)
                    g = jnp.concatenate([gw[r0:r1, place(b) * B : (place(b) + 1) * B] for b in range(a + 1, COLS)], axis=1)
                    if a:
                        g = g - dot_t(rr[0:r0, r0:r1], rr[0:r0, r1:K])
                    rr[r0:r1, r1:K] = dot(lis[a], g)
                for after in {0: (2,), 1: range(3, COLS)}.get(a, ()):
                    send_diagonal(after)
                    if after + 1 < COLS:
                        send_rows(after)
                if 1 < a + 1 < COLS - 1:
                    hand_over(a + 1)

    mine_r = k // 4

    @pl.when(n >= mine_r)
    def _():
        tv[...] = rr[own_rows, pl.ds(pl.multiple_of(n * B, B), B)]

    @pl.when(n < mine_r)
    def _():
        tv[...] = jnp.zeros_like(tv)

    local(tv, tri, m_r.at[2])

    take(dl.at[1 - core], i_r)
    for r in range(ROWS):
        rhs[32 * r : 32 * r + 32, B : 3 * B] = dl[r % 2, r // 2]
    take(rhs.at[:, 0:B], f_r)
    for a in range(COLS):
        r0, r1 = a * B, (a + 1) * B
        s = rhs[r0:r1, :]
        x = fast(lis[a], s)
        rhs[r0:r1, :] = x
        if a + 1 < COLS:
            rhs[r1:K, :] -= fast_t(rr[r0:r1, r1:K], x)
    oo[...] = fast_t(rhs[:, 0:B], rhs[:, B : 3 * B])
    result = oo.at[pl.ds(pl.multiple_of(64 * core, 64), 64)]
    local(result, out, m_r.at[3])

    take(tv, m_r.at[2])
    take(ov, m_r.at[3])
    take(zb.at[0:4], z_s)
    take(zb.at[0:3], w_s)
    for d in range(5):
        def left_share(d=d):
            @pl.when(mine[d])
            def _():
                take(rg.at[d, 0:15], g_s.at[d])
                take(rg.at[d, 0:7], y_s.at[d])

            @pl.when(jnp.logical_not(mine[d]))
            def _():
                take(rg.at[d, 0:16], g_s.at[d])

        if d < 4:
            left_share()
        else:
            pl.when(n < 4)(left_share)
    for a in range(COLS):
        @pl.when(core == a % 2)
        def _(a=a):
            take(rg.at[0, 0:31], b_s.at[a])

        for parity in range(2):
            c0, c1 = held(a, parity)
            if c0 < c1:
                @pl.when(core == parity)
                def _(a=a, c0=c0, c1=c1):
                    take(gw.at[a * B : a * B + 120, c0:c1], a_s.at[a])
                    take(gw.at[a * B : (a + 1) * B, c0:c1], p_s.at[a])
    take(qd, q_s.at[0])
    take(qc, q_s.at[1])
    take(rd.at[0:15], d_s)
    take(rc.at[0:15], c_s)
    take(rd.at[0:15], e_s)
    take(rd, i_s)
    take(cz.at[0:7], h_s)
    take(rhs.at[0 : K - 32, 0:B], f_s)


def local_step(am, bm, ap, bp):
    f32 = jnp.float32
    vmem = pltpu.VMEM
    dma = pltpu.SemaphoreType.DMA
    return pl.pallas_call(
        kernel,
        out_shape=(jax.ShapeDtypeStruct((32, B), f32), jax.ShapeDtypeStruct((64, 256), f32)),
        in_specs=[pl.BlockSpec(memory_space=pl.ANY)] * 4,
        out_specs=[pl.BlockSpec(memory_space=pl.ANY)] * 2,
        scratch_shapes=[
            vmem((64, 256), f32),
            vmem((64, 256), f32),
            vmem((32, B), f32),
            vmem((64, 256), f32),
            vmem((COLS, B, B), f32),
            vmem((5, B, B), f32),
            vmem((5, ROWS, 8, B), f32),
            vmem((5, 8, B), f32),
            vmem((COLS, 8, B), f32),
            vmem((COLS, B, B), f32),
            vmem((K, K), f32),
            vmem((2, CHIPS, 32, 256), f32),
            vmem((2, CHIPS, 32, 256), f32),
            vmem((CHIPS, 32, 256), f32),
            vmem((CHIPS, 32, 256), f32),
            vmem((CHIPS, 32, 256), f32),
            vmem((CHIPS, 32, 256), f32),
            vmem((32, 256), f32),
            vmem((32, 256), f32),
            vmem((COLS, 32, 256), f32),
            vmem((2, CHIPS, 32, 256), f32),
            vmem((K, 3 * B), f32),
            vmem((K, K), f32),
            vmem((COLS, B, B), f32),
            vmem((B, B), f32),
            vmem((B, B), f32),
            vmem((B, 256), f32),
            dma, dma((COLS,)), dma,
            dma((5,)), dma((5,)),
            dma((5,)), dma((COLS,)), dma((COLS,)),
            dma((COLS,)), dma((COLS,)),
            dma((COLS,)), dma((COLS,)),
            dma((COLS,)), dma((COLS,)),
            dma((2,)), dma((2,)),
            dma, dma, dma, dma, dma, dma, dma, dma, dma, dma, dma, dma,
            dma((CHIPS,)), dma((4,)),
        ],
        compiler_params=pltpu.CompilerParams(
            collective_id=0, has_side_effects=True, vmem_limit_bytes=60 * 2**20
        ),
    )(am, bm, ap, bp)


def solution(mesh):
    spec = P("row", "col")
    return jax.shard_map(
        local_step, mesh=mesh, in_specs=(spec,) * 4, out_specs=(spec, spec), check_vma=False
    )
```

```python
import jax
import jax.numpy as jnp
from jax import lax
from jax.experimental import pallas as pl
from jax.experimental.pallas import tpu as pltpu
from jax.sharding import PartitionSpec as P

HIGHEST = lax.Precision.HIGHEST
MESH = pl.DeviceIdType.MESH
B = 128
ROWS = 32
COLS = 8
CHIPS = 16
K = COLS * B
PAIR_C_STEP = 2
PAIR_D_STEP = 4
SUM_C_STEP = 4
SUM_D_STEP = 6
SPREAD_STEP = 6


def dot_t(a, b):
    return lax.dot_general(
        a, b, (((0,), (0,)), ((), ())), precision=HIGHEST, preferred_element_type=jnp.float32
    )


def dot(a, b):
    return jnp.dot(a, b, precision=HIGHEST, preferred_element_type=jnp.float32)


def split(x):
    high = x.astype(jnp.bfloat16)
    return high, (x - high.astype(jnp.float32)).astype(jnp.bfloat16)


def dot_split(a, b, dims):
    (ah, al), (bh, bl) = split(a), split(b)

    def part(x, y):
        return lax.dot_general(x, y, (dims, ((), ())), preferred_element_type=jnp.float32)

    return part(ah, bh) + (part(ah, bl) + part(al, bh))


def fast_t(a, b):
    return dot_split(a, b, ((0,), (0,)))


def fast(a, b):
    return dot_split(a, b, ((1,), (0,)))


def lane(x, k):
    return jnp.broadcast_to(x[:, k : k + 1], x.shape)


def sub(x, k):
    return jnp.broadcast_to(x[k : k + 1, :], x.shape)


def total(terms):
    while len(terms) > 1:
        odd = terms[len(terms) - len(terms) % 2 :]
        terms = [terms[m] + terms[m + 1] for m in range(0, len(terms) - 1, 2)] + odd
    return terms[0]


def factor_block(d_ref, r_ref, li_ref):
    srow = lax.broadcasted_iota(jnp.int32, (8, B), 0)
    lcol = lax.broadcasted_iota(jnp.int32, (8, B), 1)
    groups = B // 8
    left = [d_ref[8 * g : 8 * g + 8, :] for g in range(groups)]
    right = [jnp.where(lcol == srow + 8 * g, 1.0, 0.0).astype(jnp.float32) for g in range(groups)]
    cols = [lane(left[0], m) for m in range(8)]
    for i in range(groups):
        p, q = left[i], right[i]
        more = i + 1 < groups
        ahead = []
        if more:
            by = [lane(left[i + 1], 8 * i + m) for m in range(8)]
            later = [lane(left[i + 1], 8 * i + 8 + m) for m in range(8)]
            ahead = [lane(p, 8 * i + 8 + m) for m in range(8)]
        rp = jnp.zeros((8, B), jnp.float32)
        rq = rp
        for m in range(8):
            pivot = sub(cols[m], m)
            inv = 1.0 / pivot
            root = lax.rsqrt(pivot)
            f = jnp.where(srow == m, 1.0 - inv, cols[m] * inv)
            for c in range(m + 1, 8):
                cols[c] = cols[c] - f * sub(cols[c], m)
            pm, qm = sub(p, m), sub(q, m)
            rp = jnp.where(srow == m, pm * root, rp)
            rq = jnp.where(srow == m, qm * root, rq)
            p = p - f * pm
            q = q - f * qm
            ahead = [x - f * sub(x, m) for x in ahead]
        r_ref[8 * i : 8 * i + 8, :] = jnp.where(lcol >= srow + 8 * i, rp, 0.0)
        li_ref[8 * i : 8 * i + 8, :] = rq
        yp = [sub(p, m) for m in range(8)]
        yq = [sub(q, m) for m in range(8)]
        if more:
            cols = [later[c] - total([by[m] * sub(ahead[c], m) for m in range(8)]) for c in range(8)]
        for g in range(i + 1, groups):
            w = by if g == i + 1 else [lane(left[g], 8 * i + m) for m in range(8)]
            left[g] = left[g] - total([w[m] * yp[m] for m in range(8)])
            right[g] = right[g] - total([w[m] * yq[m] for m in range(8)])


def place(b):
    return b // 2 + 4 * (b % 2)


def held(a, parity):
    first = a + 1 if (a + 1) % 2 == parity else a + 2
    return (first // 2 + 4 * parity) * B, (4 + 4 * parity) * B


def kernel(
    am, bm, ap, bp, tri, out,
    av, bv, tv, zb, pg, rg, sg, gc, gd, gw, pd, pcx, qd, qc, rd, rc, sd, sc, cz, rhs, rr, lis, dd, dr, oo,
    z_s, z_r, w_s, g_s, g_r, y_s, y_r, yd_r, b_s, b_r, a_s, a_r, p_s, p_r,
    q_s, q_r, d_s, d_r, c_s, c_r, e_s, e_r, h_s, h_r, f_s, f_r, i_s, i_r, o_r, m_r,
):
    k = lax.axis_index("row")
    n = lax.axis_index("col")
    t = k // 2
    core = lax.rem(k, 2)

    pltpu.make_async_copy(am, av, m_r.at[0]).start()
    pltpu.make_async_copy(bm, bv, m_r.at[1]).start()
    barrier = pltpu.get_barrier_semaphore()
    for s in range(1, COLS):
        pl.semaphore_signal(barrier, inc=1, device_id=(k, lax.rem(n + s, COLS)), device_id_type=MESH)
    for s in range(1, ROWS):
        pl.semaphore_signal(barrier, inc=1, device_id=(lax.rem(k + s, ROWS), n), device_id_type=MESH)
    pl.semaphore_wait(barrier, COLS - 1 + ROWS - 1)

    def send(src, dst, ssem, rsem, row, col):
        pltpu.make_async_remote_copy(
            src_ref=src, dst_ref=dst, send_sem=ssem, recv_sem=rsem, device_id=(row, col), device_id_type=MESH
        ).start()

    def local(src, dst, sem):
        pltpu.make_async_copy(src, dst, sem).start()

    def take(ref, sem):
        pltpu.make_async_copy(ref, ref, sem).wait()

    def near(s):
        return lax.rem(n + s + COLS, COLS)

    def send_panels(steps, sem):
        for s in steps:
            send(bp, zb.at[n, 0:64], sem, z_r.at[n], k, near(s))
            send(ap, zb.at[n, 64:128], sem, z_r.at[n], k, near(s))

    send_panels((1, -1, 2, -2), z_s)
    local(bp, zb.at[n, 0:64], z_r.at[n])
    local(ap, zb.at[n, 64:128], z_r.at[n])
    lows, highs, mine = [], [], []
    for d in range(5):
        i, j = near(-(d // 2)), near((d + 1) // 2)
        lo, hi = jnp.minimum(i, j), jnp.maximum(i, j)
        lows.append(lo)
        highs.append(hi)
        mine.append(lax.rem(hi, 2) == core)

    def where_needed(d, body):
        if d < 4:
            body()
        else:
            pl.when(n < 4)(body)

    def share(d):
        def body():
            pg[d] = dot_t(zb[lows[d]], zb[highs[d]])
            to_core = lax.rem(highs[d], 2)
            for s in range(1, CHIPS):
                to = lax.rem(t + s, CHIPS)
                send(pg.at[d, pl.ds(pl.multiple_of(8 * to, 8), 8)], rg.at[d, k], g_s.at[d], g_r.at[d], 2 * to + to_core, n)
            own = pg.at[d, pl.ds(pl.multiple_of(8 * t, 8), 8)]

            @pl.when(mine[d])
            def _():
                local(own, rg.at[d, k], g_r.at[d])

            @pl.when(jnp.logical_not(mine[d]))
            def _():
                send(own, rg.at[d, k], g_s.at[d], g_r.at[d], 2 * t + 1 - core, n)

        where_needed(d, body)

    def add_up(d):
        def body():
            @pl.when(mine[d])
            def _():
                take(rg.at[d], g_r.at[d])
                sg[d] = jnp.sum(rg[d], axis=0)
                if d == 0:
                    there, sem = gc.at[n], yd_r.at[n]
                else:
                    row = pl.ds(pl.multiple_of(lows[d] * B + 8 * t, 8), 8)
                    pos = highs[d] // 2 + 4 * core
                    there, sem = gw.at[row, pl.ds(pl.multiple_of(pos * B, B), B)], y_r.at[lows[d]]
                local(sg.at[d], there, sem)
                for s in (1, -1, 2, -2, 3, -3, 4):
                    send(sg.at[d], there, y_s.at[d], sem, k, near(s))

        where_needed(d, body)

    rows8 = pl.ds(pl.multiple_of(8 * t, 8), 8)

    def send_diagonal(a):
        @pl.when(core == a % 2)
        def _():
            take(gc.at[a], yd_r.at[a])
            for s in range(1, ROWS):
                send(gc.at[a], gd.at[a, rows8], b_s.at[a], b_r.at[a], lax.rem(k + s, ROWS), n)
            local(gc.at[a], gd.at[a, rows8], b_r.at[a])

    def send_rows(a):
        for parity in range(2):
            c0, c1 = held(a, parity)
            if c0 < c1:
                @pl.when(core == parity)
                def _(c0=c0, c1=c1):
                    piece = gw.at[pl.ds(pl.multiple_of(a * B + 8 * t, 8), 8), c0:c1]
                    take(piece, y_r.at[a])
                    for s in range(1, CHIPS):
                        sem = a_r.at[a] if a else o_r.at[s]
                        to = 2 * lax.rem(t + s, CHIPS)
                        send(piece, piece, a_s.at[a], sem, to + core, n)
                        if a in (1, 2):
                            send(piece, piece, p_s.at[a], p_r.at[a], to + 1 - core, n)
                    if a < 3:
                        send(piece, piece, p_s.at[a], p_r.at[a], k + 1 - 2 * core, n)

    take(zb.at[n], z_r.at[n])
    share(0)
    take(zb.at[near(1)], z_r.at[near(1)])
    share(1)
    add_up(0)
    take(zb.at[near(-1)], z_r.at[near(-1)])
    share(2)
    take(zb.at[near(2)], z_r.at[near(2)])
    share(3)
    take(zb.at[near(-2)], z_r.at[near(-2)])
    share(4)
    send_panels((3, -3, 4), w_s)
    send_diagonal(0)
    for d in range(1, 5):
        add_up(d)

    def form_products():
        take(av, m_r.at[0])
        take(bv, m_r.at[1])
        for s in (3, -3, 4):
            take(zb.at[near(s)], z_r.at[near(s)])
        for c in range(COLS):
            d_part = fast_t(zb[c, 64:128, :], bv[...])
            c_part = fast_t(zb[c, 0:64, :], av[...])
            for e in range(4):
                r = 4 * c + e
                pd[r % 2, r // 2] = d_part[32 * e : 32 * e + 32, :]
                pcx[r % 2, r // 2] = c_part[32 * e : 32 * e + 32, :]
        send(pcx.at[1 - core], qc, q_s.at[1], q_r.at[1], k + 1 - 2 * core, n)
        send(pd.at[1 - core], qd, q_s.at[0], q_r.at[0], k + 1 - 2 * core, n)

    own_rows = pl.ds(pl.multiple_of(32 * k, 32), 32)

    def hand_over(a):
        for parity in range(2):
            c0, c1 = held(a, parity)
            if c0 < c1:
                @pl.when(core == parity)
                def _(c0=c0, c1=c1):
                    if a == 0:
                        for s in range(1, CHIPS):
                            source = lax.rem(t - s + CHIPS, CHIPS)
                            piece = gw.at[pl.ds(pl.multiple_of(8 * source, 8), 8), c0:c1]
                            take(piece, o_r.at[s])
                            send(piece, piece, p_s.at[a], p_r.at[a], k + 1 - 2 * core, n)
                    else:
                        take(gw.at[a * B : a * B + 120, c0:c1], a_r.at[a])
                    if a > 2:
                        panel = gw.at[a * B : (a + 1) * B, c0:c1]
                        send(panel, panel, p_s.at[a], p_r.at[a], k + 1 - 2 * core, n)

    def arrived(a):
        for parity in range(2):
            c0, c1 = held(a, parity)
            if c0 < c1:
                @pl.when(core != parity)
                def _(c0=c0, c1=c1):
                    take(gw.at[a * B : (a + 1) * B, c0:c1], p_r.at[a])

    def pair_up(index, got, ours, there, ssem, rsem):
        take(got, q_r.at[index])
        got[...] += ours[core]
        for s in range(1, CHIPS):
            to = lax.rem(t + s, CHIPS)
            send(got.at[to], there.at[t], ssem, rsem, 2 * to + core, n)
        local(got.at[t], there.at[t], rsem)

    def sum_c():
        take(rc, c_r)
        sc[...] = jnp.sum(rc[...], axis=0)
        for s in (1, -1, 2, -2, 3, -3, 4):
            send(sc, cz.at[n], h_s, h_r, k, near(s))
        local(sc, cz.at[n], h_r)

    def sum_d():
        take(rd, d_r)
        sd[...] = jnp.sum(rd[...], axis=0)
        there = rhs.at[own_rows, B : 2 * B]
        for s in range(1, ROWS):
            to = lax.rem(k + s, ROWS)
            send(sd.at[:, pl.ds(pl.multiple_of(lax.rem(to, 2) * B, B), B)], there, e_s, e_r, to, n)
        local(sd.at[:, pl.ds(pl.multiple_of(core * B, B), B)], there, e_r)

    def spread_products():
        take(cz, h_r)
        for s in range(ROWS):
            to = lax.rem(k + s, ROWS)
            half = pl.ds(pl.multiple_of(lax.rem(to // 2, 2) * B, B), B)
            piece, there = cz.at[to // 4, :, half], rhs.at[own_rows, 0:B]
            if s:
                send(piece, there, f_s, f_r, to, n)
            else:
                local(piece, there, f_r)

    def blocks(a):
        row = slice(a * B, (a + 1) * B)
        rest = [gw[row, place(b) * B : (place(b) + 1) * B] for b in range(a + 1, COLS)]
        return jnp.concatenate([gd[a]] + rest, axis=1)

    @pl.loop(0, COLS)
    def _(p):
        for a in range(COLS):
            @pl.when(p == a)
            def _(a=a):
                if a == PAIR_C_STEP:
                    pair_up(1, qc, pcx, rc, c_s, c_r)
                if a == PAIR_D_STEP:
                    pair_up(0, qd, pd, rd, d_s, d_r)
                if a == SUM_D_STEP:
                    sum_d()
                take(gd.at[a], b_r.at[a])
                r0, r1 = a * B, (a + 1) * B
                if a:
                    u = rr[0:r0, r0:r1]
                    dd[...] = gd[a] - dot_t(u, u)
                else:
                    dd[...] = gd[0]
        factor_block(dd, dr, lis.at[p])
        for a in range(COLS):
            @pl.when(p == a)
            def _(a=a):
                r0, r1 = a * B, (a + 1) * B
                if a == SUM_C_STEP:
                    sum_c()
                if a == SPREAD_STEP:
                    spread_products()
                rr[r0:r1, r0:r1] = dr[...]
                if a + 1 < COLS:
                    if a == 0:
                        send_rows(0)
                        form_products()
                        send_diagonal(1)
                        send_rows(1)
                        hand_over(0)
                    if a in (1, 2):
                        hand_over(a)
                    arrived(a)
                    if a:
                        g = blocks(a)[:, B:] - dot_t(rr[0:r0, r0:r1], rr[0:r0, r1:K])
                    else:
                        g = blocks(a)[:, B:]
                    rr[r0:r1, r1:K] = dot(lis[a], g)
                for after in {0: (2,), 1: range(3, COLS)}.get(a, ()):
                    send_diagonal(after)
                    if after + 1 < COLS:
                        send_rows(after)
                for after in {2: (3,), 3: (4,), 4: (5,), 5: (6,)}.get(a, ()):
                    hand_over(after)

    mine_r = k // 4

    @pl.when(n >= mine_r)
    def _():
        tv[...] = rr[own_rows, pl.ds(pl.multiple_of(n * B, B), B)]

    @pl.when(n < mine_r)
    def _():
        tv[...] = jnp.zeros_like(tv)

    local(tv, tri, m_r.at[2])

    take(rhs.at[:, B : 2 * B], e_r)
    for a in range(COLS):
        r0, r1 = a * B, (a + 1) * B
        x = fast(lis[a], rhs[r0:r1, B : 2 * B])
        rhs[r0:r1, B : 2 * B] = x
        if a + 1 < COLS:
            rhs[r1:K, B : 2 * B] -= fast_t(rr[r0:r1, r1:K], x)
    for a in reversed(range(COLS)):
        r0, r1 = a * B, (a + 1) * B
        x = rhs[r0:r1, B : 2 * B]
        if a + 1 < COLS:
            x = x - fast(rr[r0:r1, r1:K], rhs[r1:K, B : 2 * B])
        rhs[r0:r1, B : 2 * B] = fast_t(lis[a], x)
    take(rhs.at[:, 0:B], f_r)
    oo[...] = fast_t(rhs[:, 0:B], rhs[:, B : 2 * B])
    half = out.at[:, pl.ds(pl.multiple_of(core * B, B), B)]
    send(oo.at[pl.ds(pl.multiple_of(64 * (1 - core), 64), 64)], half, i_s, i_r, k + 1 - 2 * core, n)
    local(oo.at[pl.ds(pl.multiple_of(64 * core, 64), 64)], half, m_r.at[3])

    take(tv, m_r.at[2])
    take(oo.at[0:64], m_r.at[3])
    take(oo.at[0:64], i_r)
    take(oo.at[0:64], i_s)
    take(zb.at[0:4], z_s)
    take(zb.at[0:3], w_s)
    for d in range(5):
        def left_share(d=d):
            @pl.when(mine[d])
            def _():
                take(rg.at[d, 0:15], g_s.at[d])
                take(rg.at[d, 0:7], y_s.at[d])

            @pl.when(jnp.logical_not(mine[d]))
            def _():
                take(rg.at[d, 0:16], g_s.at[d])

        if d < 4:
            left_share()
        else:
            pl.when(n < 4)(left_share)
    for a in range(COLS):
        @pl.when(core == a % 2)
        def _(a=a):
            take(rg.at[0, 0:31], b_s.at[a])

        for parity in range(2):
            c0, c1 = held(a, parity)
            if c0 < c1:
                @pl.when(core == parity)
                def _(a=a, c0=c0, c1=c1):
                    take(gw.at[a * B : a * B + 120, c0:c1], a_s.at[a])
                    take(gw.at[a * B : (a + 1) * B, c0:c1], p_s.at[a])
    take(qd, q_s.at[0])
    take(qc, q_s.at[1])
    take(rd.at[0:15], d_s)
    take(rc.at[0:15], c_s)
    take(rhs.at[0 : K - 32, B : 2 * B], e_s)
    take(cz.at[0:7], h_s)
    take(rhs.at[0 : K - 32, 0:B], f_s)


def hand_on(tri, cross, tri_out, cross_out):
    tri_out[...] = tri[...]
    cross_out[...] = cross[...]


def local_step(am, bm, ap, bp):
    f32 = jnp.float32
    vmem = pltpu.VMEM
    dma = pltpu.SemaphoreType.DMA
    results = pl.pallas_call(
        kernel,
        out_shape=(jax.ShapeDtypeStruct((32, B), f32), jax.ShapeDtypeStruct((64, 256), f32)),
        in_specs=[pl.BlockSpec(memory_space=pl.ANY)] * 4,
        out_specs=[pl.BlockSpec(memory_space=pl.ANY)] * 2,
        scratch_shapes=[
            vmem((64, 256), f32),
            vmem((64, 256), f32),
            vmem((32, B), f32),
            vmem((COLS, B, B), f32),
            vmem((5, B, B), f32),
            vmem((5, ROWS, 8, B), f32),
            vmem((5, 8, B), f32),
            vmem((COLS, 8, B), f32),
            vmem((COLS, B, B), f32),
            vmem((K, K), f32),
            vmem((2, CHIPS, 32, 256), f32),
            vmem((2, CHIPS, 32, 256), f32),
            vmem((CHIPS, 32, 256), f32),
            vmem((CHIPS, 32, 256), f32),
            vmem((CHIPS, 32, 256), f32),
            vmem((CHIPS, 32, 256), f32),
            vmem((32, 256), f32),
            vmem((32, 256), f32),
            vmem((COLS, 32, 256), f32),
            vmem((K, 2 * B), f32),
            vmem((K, K), f32),
            vmem((COLS, B, B), f32),
            vmem((B, B), f32),
            vmem((B, B), f32),
            vmem((B, B), f32),
            dma, dma((COLS,)), dma,
            dma((5,)), dma((5,)),
            dma((5,)), dma((COLS,)), dma((COLS,)),
            dma((COLS,)), dma((COLS,)),
            dma((COLS,)), dma((COLS,)),
            dma((COLS,)), dma((COLS,)),
            dma((2,)), dma((2,)),
            dma, dma, dma, dma, dma, dma, dma, dma, dma, dma, dma, dma,
            dma((CHIPS,)), dma((4,)),
        ],
        compiler_params=pltpu.CompilerParams(
            collective_id=0, has_side_effects=True, vmem_limit_bytes=60 * 2**20
        ),
    )(am, bm, ap, bp)
    return pl.pallas_call(
        hand_on,
        out_shape=(jax.ShapeDtypeStruct((32, B), f32), jax.ShapeDtypeStruct((64, 256), f32)),
        in_specs=[pl.BlockSpec(memory_space=vmem)] * 2,
        out_specs=[pl.BlockSpec(memory_space=vmem)] * 2,
    )(*results)


def solution(mesh):
    spec = P("row", "col")
    return jax.shard_map(
        local_step, mesh=mesh, in_specs=(spec,) * 4, out_specs=(spec, spec), check_vma=False
    )
```

```python
import jax
import jax.numpy as jnp
from jax import lax
from jax.experimental import pallas as pl
from jax.experimental.pallas import tpu as pltpu
from jax.sharding import PartitionSpec as P

HIGHEST = lax.Precision.HIGHEST
MESH = pl.DeviceIdType.MESH
B = 128
ROWS = 32
COLS = 8
CHIPS = 16
K = COLS * B
PAIR_C_STEP = 1
PAIR_D_STEP = 3
SUM_C_STEP = 4
SUM_D_STEP = 5
SPREAD_STEP = 5


def dot_t(a, b):
    return lax.dot_general(
        a, b, (((0,), (0,)), ((), ())), precision=HIGHEST, preferred_element_type=jnp.float32
    )


def dot(a, b):
    return jnp.dot(a, b, precision=HIGHEST, preferred_element_type=jnp.float32)


def split(x):
    high = x.astype(jnp.bfloat16)
    return high, (x - high.astype(jnp.float32)).astype(jnp.bfloat16)


def dot_split(a, b, dims):
    (ah, al), (bh, bl) = split(a), split(b)

    def part(x, y):
        return lax.dot_general(x, y, (dims, ((), ())), preferred_element_type=jnp.float32)

    return part(ah, bh) + (part(ah, bl) + part(al, bh))


def fast_t(a, b):
    return dot_split(a, b, ((0,), (0,)))


def fast(a, b):
    return dot_split(a, b, ((1,), (0,)))


def lane(x, k):
    return jnp.broadcast_to(x[:, k : k + 1], x.shape)


def sub(x, k):
    return jnp.broadcast_to(x[k : k + 1, :], x.shape)


def total(terms):
    while len(terms) > 1:
        odd = terms[len(terms) - len(terms) % 2 :]
        terms = [terms[m] + terms[m + 1] for m in range(0, len(terms) - 1, 2)] + odd
    return terms[0]


def factor_block(d_ref, r_ref, li_ref):
    srow = lax.broadcasted_iota(jnp.int32, (8, B), 0)
    lcol = lax.broadcasted_iota(jnp.int32, (8, B), 1)
    groups = B // 8
    left = [d_ref[8 * g : 8 * g + 8, :] for g in range(groups)]
    right = [jnp.where(lcol == srow + 8 * g, 1.0, 0.0).astype(jnp.float32) for g in range(groups)]
    cols = [lane(left[0], m) for m in range(8)]
    for i in range(groups):
        p, q = left[i], right[i]
        more = i + 1 < groups
        ahead = []
        if more:
            by = [lane(left[i + 1], 8 * i + m) for m in range(8)]
            later = [lane(left[i + 1], 8 * i + 8 + m) for m in range(8)]
            ahead = [lane(p, 8 * i + 8 + m) for m in range(8)]
        rp = jnp.zeros((8, B), jnp.float32)
        rq = rp
        for m in range(8):
            pivot = sub(cols[m], m)
            inv = 1.0 / pivot
            root = lax.rsqrt(pivot)
            f = jnp.where(srow == m, 1.0 - inv, cols[m] * inv)
            for c in range(m + 1, 8):
                cols[c] = cols[c] - f * sub(cols[c], m)
            pm, qm = sub(p, m), sub(q, m)
            rp = jnp.where(srow == m, pm * root, rp)
            rq = jnp.where(srow == m, qm * root, rq)
            p = p - f * pm
            q = q - f * qm
            ahead = [x - f * sub(x, m) for x in ahead]
        r_ref[8 * i : 8 * i + 8, :] = jnp.where(lcol >= srow + 8 * i, rp, 0.0)
        li_ref[8 * i : 8 * i + 8, :] = rq
        yp = [sub(p, m) for m in range(8)]
        yq = [sub(q, m) for m in range(8)]
        if more:
            cols = [later[c] - total([by[m] * sub(ahead[c], m) for m in range(8)]) for c in range(8)]
        for g in range(i + 1, groups):
            w = by if g == i + 1 else [lane(left[g], 8 * i + m) for m in range(8)]
            left[g] = left[g] - total([w[m] * yp[m] for m in range(8)])
            right[g] = right[g] - total([w[m] * yq[m] for m in range(8)])


def place(b):
    return b // 2 + 4 * (b % 2)


def held(a, parity):
    first = a + 1 if (a + 1) % 2 == parity else a + 2
    return (first // 2 + 4 * parity) * B, (4 + 4 * parity) * B


def kernel(
    am, bm, ap, bp, tri, out,
    av, bv, tv, zb, pg, rg, sg, gc, gd, gw, pd, pcx, qd, qc, rd, rc, sd, sc, cz, rhs, rr, lis, dd, dr, oo,
    z_s, z_r, w_s, g_s, g_r, y_s, y_r, yd_r, b_s, b_r, a_s, a_r, p_s, p_r,
    q_s, q_r, d_s, d_r, c_s, c_r, e_s, e_r, h_s, h_r, f_s, f_r, i_s, i_r, o_r, m_r,
):
    k = lax.axis_index("row")
    n = lax.axis_index("col")
    t = k // 2
    core = lax.rem(k, 2)

    pltpu.make_async_copy(am, av, m_r.at[0]).start()
    pltpu.make_async_copy(bm, bv, m_r.at[1]).start()
    barrier = pltpu.get_barrier_semaphore()
    for s in range(1, COLS):
        pl.semaphore_signal(barrier, inc=1, device_id=(k, lax.rem(n + s, COLS)), device_id_type=MESH)
    for s in range(1, ROWS):
        pl.semaphore_signal(barrier, inc=1, device_id=(lax.rem(k + s, ROWS), n), device_id_type=MESH)
    pl.semaphore_wait(barrier, COLS - 1 + ROWS - 1)

    def send(src, dst, ssem, rsem, row, col):
        pltpu.make_async_remote_copy(
            src_ref=src, dst_ref=dst, send_sem=ssem, recv_sem=rsem, device_id=(row, col), device_id_type=MESH
        ).start()

    def local(src, dst, sem):
        pltpu.make_async_copy(src, dst, sem).start()

    def take(ref, sem):
        pltpu.make_async_copy(ref, ref, sem).wait()

    def near(s):
        return lax.rem(n + s + COLS, COLS)

    def send_panels(steps, sem):
        for s in steps:
            send(bp, zb.at[n, 0:64], sem, z_r.at[n], k, near(s))
            send(ap, zb.at[n, 64:128], sem, z_r.at[n], k, near(s))

    send_panels((1, -1, 2, -2), z_s)
    local(bp, zb.at[n, 0:64], z_r.at[n])
    local(ap, zb.at[n, 64:128], z_r.at[n])
    lows, highs, mine = [], [], []
    for d in range(5):
        i, j = near(-(d // 2)), near((d + 1) // 2)
        lo, hi = jnp.minimum(i, j), jnp.maximum(i, j)
        lows.append(lo)
        highs.append(hi)
        mine.append(lax.rem(hi, 2) == core)

    def where_needed(d, body):
        if d < 4:
            body()
        else:
            pl.when(n < 4)(body)

    def share(d):
        def body():
            pg[d] = dot_t(zb[lows[d]], zb[highs[d]])
            to_core = lax.rem(highs[d], 2)
            for s in range(1, CHIPS):
                to = lax.rem(t + s, CHIPS)
                send(pg.at[d, pl.ds(pl.multiple_of(8 * to, 8), 8)], rg.at[d, k], g_s.at[d], g_r.at[d], 2 * to + to_core, n)
            own = pg.at[d, pl.ds(pl.multiple_of(8 * t, 8), 8)]

            @pl.when(mine[d])
            def _():
                local(own, rg.at[d, k], g_r.at[d])

            @pl.when(jnp.logical_not(mine[d]))
            def _():
                send(own, rg.at[d, k], g_s.at[d], g_r.at[d], 2 * t + 1 - core, n)

        where_needed(d, body)

    def add_up(d):
        def body():
            @pl.when(mine[d])
            def _():
                take(rg.at[d], g_r.at[d])
                sg[d] = jnp.sum(rg[d], axis=0)
                if d == 0:
                    there, sem = gc.at[n], yd_r.at[n]
                else:
                    row = pl.ds(pl.multiple_of(lows[d] * B + 8 * t, 8), 8)
                    pos = highs[d] // 2 + 4 * core
                    there, sem = gw.at[row, pl.ds(pl.multiple_of(pos * B, B), B)], y_r.at[lows[d]]
                local(sg.at[d], there, sem)
                for s in (1, -1, 2, -2, 3, -3, 4):
                    send(sg.at[d], there, y_s.at[d], sem, k, near(s))

        where_needed(d, body)

    rows8 = pl.ds(pl.multiple_of(8 * t, 8), 8)

    def send_diagonal(a):
        @pl.when(core == a % 2)
        def _():
            take(gc.at[a], yd_r.at[a])
            for s in range(1, ROWS):
                send(gc.at[a], gd.at[a, rows8], b_s.at[a], b_r.at[a], lax.rem(k + s, ROWS), n)
            local(gc.at[a], gd.at[a, rows8], b_r.at[a])

    def send_rows(a):
        for parity in range(2):
            c0, c1 = held(a, parity)
            if c0 < c1:
                @pl.when(core == parity)
                def _(c0=c0, c1=c1):
                    piece = gw.at[pl.ds(pl.multiple_of(a * B + 8 * t, 8), 8), c0:c1]
                    take(piece, y_r.at[a])
                    for s in range(1, CHIPS):
                        sem = a_r.at[a] if a else o_r.at[s]
                        to = 2 * lax.rem(t + s, CHIPS)
                        send(piece, piece, a_s.at[a], sem, to + core, n)
                        if a == 1:
                            send(piece, piece, p_s.at[a], p_r.at[a], to + 1 - core, n)
                    if a < 2:
                        send(piece, piece, p_s.at[a], p_r.at[a], k + 1 - 2 * core, n)

    take(zb.at[n], z_r.at[n])
    share(0)
    take(zb.at[near(1)], z_r.at[near(1)])
    share(1)
    add_up(0)
    take(zb.at[near(-1)], z_r.at[near(-1)])
    share(2)
    take(zb.at[near(2)], z_r.at[near(2)])
    share(3)
    take(zb.at[near(-2)], z_r.at[near(-2)])
    share(4)
    send_panels((3, -3, 4), w_s)
    send_diagonal(0)
    for d in range(1, 5):
        add_up(d)

    def form_products():
        take(av, m_r.at[0])
        take(bv, m_r.at[1])
        for s in (3, -3, 4):
            take(zb.at[near(s)], z_r.at[near(s)])
        for c in range(COLS):
            d_part = fast_t(zb[c, 64:128, :], bv[...])
            c_part = fast_t(zb[c, 0:64, :], av[...])
            for e in range(4):
                r = 4 * c + e
                pd[r % 2, r // 2] = d_part[32 * e : 32 * e + 32, :]
                pcx[r % 2, r // 2] = c_part[32 * e : 32 * e + 32, :]
        send(pcx.at[1 - core], qc, q_s.at[1], q_r.at[1], k + 1 - 2 * core, n)
        send(pd.at[1 - core], qd, q_s.at[0], q_r.at[0], k + 1 - 2 * core, n)

    own_rows = pl.ds(pl.multiple_of(32 * k, 32), 32)

    def hand_over(a):
        for parity in range(2):
            c0, c1 = held(a, parity)
            if c0 < c1:
                @pl.when(core == parity)
                def _(c0=c0, c1=c1):
                    if a == 0:
                        for s in range(1, CHIPS):
                            source = lax.rem(t - s + CHIPS, CHIPS)
                            piece = gw.at[pl.ds(pl.multiple_of(8 * source, 8), 8), c0:c1]
                            take(piece, o_r.at[s])
                            send(piece, piece, p_s.at[a], p_r.at[a], k + 1 - 2 * core, n)
                    else:
                        take(gw.at[a * B : a * B + 120, c0:c1], a_r.at[a])
                    if a > 1:
                        panel = gw.at[a * B : (a + 1) * B, c0:c1]
                        send(panel, panel, p_s.at[a], p_r.at[a], k + 1 - 2 * core, n)

    def arrived(a):
        for parity in range(2):
            c0, c1 = held(a, parity)
            if c0 < c1:
                @pl.when(core != parity)
                def _(c0=c0, c1=c1):
                    take(gw.at[a * B : (a + 1) * B, c0:c1], p_r.at[a])

    def pair_up(index, got, ours, there, ssem, rsem):
        take(got, q_r.at[index])
        got[...] += ours[core]
        for s in range(1, CHIPS):
            to = lax.rem(t + s, CHIPS)
            send(got.at[to], there.at[t], ssem, rsem, 2 * to + core, n)
        local(got.at[t], there.at[t], rsem)

    def sum_c():
        take(rc, c_r)
        sc[...] = jnp.sum(rc[...], axis=0)
        for s in (1, -1, 2, -2, 3, -3, 4):
            send(sc, cz.at[n], h_s, h_r, k, near(s))
        local(sc, cz.at[n], h_r)

    def sum_d():
        take(rd, d_r)
        sd[...] = jnp.sum(rd[...], axis=0)
        there = rhs.at[own_rows, B : 2 * B]
        for s in range(1, ROWS):
            to = lax.rem(k + s, ROWS)
            send(sd.at[:, pl.ds(pl.multiple_of(lax.rem(to, 2) * B, B), B)], there, e_s, e_r, to, n)
        local(sd.at[:, pl.ds(pl.multiple_of(core * B, B), B)], there, e_r)

    def spread_products():
        take(cz, h_r)
        for s in range(ROWS):
            to = lax.rem(k + s, ROWS)
            half = pl.ds(pl.multiple_of(lax.rem(to // 2, 2) * B, B), B)
            piece, there = cz.at[to // 4, :, half], rhs.at[own_rows, 0:B]
            if s:
                send(piece, there, f_s, f_r, to, n)
            else:
                local(piece, there, f_r)

    def blocks(a):
        row = slice(a * B, (a + 1) * B)
        rest = [gw[row, place(b) * B : (place(b) + 1) * B] for b in range(a + 1, COLS)]
        return jnp.concatenate([gd[a]] + rest, axis=1)

    @pl.loop(0, COLS)
    def _(p):
        for a in range(COLS):
            @pl.when(p == a)
            def _(a=a):
                if a == PAIR_C_STEP:
                    pair_up(1, qc, pcx, rc, c_s, c_r)
                if a == PAIR_D_STEP:
                    pair_up(0, qd, pd, rd, d_s, d_r)
                if a == SUM_C_STEP:
                    sum_c()
                if a == SUM_D_STEP:
                    sum_d()
                take(gd.at[a], b_r.at[a])
                r0, r1 = a * B, (a + 1) * B
                if a:
                    u = rr[0:r0, r0:r1]
                    dd[...] = gd[a] - dot_t(u, u)
                else:
                    dd[...] = gd[0]
        factor_block(dd, dr, lis.at[p])
        for a in range(COLS):
            @pl.when(p == a)
            def _(a=a):
                r0, r1 = a * B, (a + 1) * B
                if a == SPREAD_STEP:
                    spread_products()
                rr[r0:r1, r0:r1] = dr[...]
                if a + 1 < COLS:
                    if a == 0:
                        send_rows(0)
                        form_products()
                        send_diagonal(1)
                        send_rows(1)
                        hand_over(0)
                    if a == 1:
                        hand_over(a)
                    arrived(a)
                    if a:
                        g = blocks(a)[:, B:] - dot_t(rr[0:r0, r0:r1], rr[0:r0, r1:K])
                    else:
                        g = blocks(a)[:, B:]
                    rr[r0:r1, r1:K] = dot(lis[a], g)
                for after in {0: (2,), 1: range(3, COLS)}.get(a, ()):
                    send_diagonal(after)
                    if after + 1 < COLS:
                        send_rows(after)
                for after in {1: (2,), 2: (3,), 3: (4,), 4: (5,), 5: (6,)}.get(a, ()):
                    hand_over(after)

    mine_r = k // 4

    @pl.when(n >= mine_r)
    def _():
        tv[...] = rr[own_rows, pl.ds(pl.multiple_of(n * B, B), B)]

    @pl.when(n < mine_r)
    def _():
        tv[...] = jnp.zeros_like(tv)

    local(tv, tri, m_r.at[2])

    take(rhs.at[:, B : 2 * B], e_r)
    take(rhs.at[:, 0:B], f_r)
    for a in range(COLS):
        r0, r1 = a * B, (a + 1) * B
        x = fast(lis[a], rhs[r0:r1, :])
        rhs[r0:r1, :] = x
        if a + 1 < COLS:
            rhs[r1:K, :] -= fast_t(rr[r0:r1, r1:K], x)
    oo[...] = fast_t(rhs[:, 0:B], rhs[:, B : 2 * B])
    half = out.at[:, pl.ds(pl.multiple_of(core * B, B), B)]
    send(oo.at[pl.ds(pl.multiple_of(64 * (1 - core), 64), 64)], half, i_s, i_r, k + 1 - 2 * core, n)
    local(oo.at[pl.ds(pl.multiple_of(64 * core, 64), 64)], half, m_r.at[3])

    take(tv, m_r.at[2])
    take(oo.at[0:64], m_r.at[3])
    take(oo.at[0:64], i_r)
    take(oo.at[0:64], i_s)
    take(zb.at[0:4], z_s)
    take(zb.at[0:3], w_s)
    for d in range(5):
        def left_share(d=d):
            @pl.when(mine[d])
            def _():
                take(rg.at[d, 0:15], g_s.at[d])
                take(rg.at[d, 0:7], y_s.at[d])

            @pl.when(jnp.logical_not(mine[d]))
            def _():
                take(rg.at[d, 0:16], g_s.at[d])

        if d < 4:
            left_share()
        else:
            pl.when(n < 4)(left_share)
    for a in range(COLS):
        @pl.when(core == a % 2)
        def _(a=a):
            take(rg.at[0, 0:31], b_s.at[a])

        for parity in range(2):
            c0, c1 = held(a, parity)
            if c0 < c1:
                @pl.when(core == parity)
                def _(a=a, c0=c0, c1=c1):
                    take(gw.at[a * B : a * B + 120, c0:c1], a_s.at[a])
                    take(gw.at[a * B : (a + 1) * B, c0:c1], p_s.at[a])
    take(qd, q_s.at[0])
    take(qc, q_s.at[1])
    take(rd.at[0:15], d_s)
    take(rc.at[0:15], c_s)
    take(rhs.at[0 : K - 32, B : 2 * B], e_s)
    take(cz.at[0:7], h_s)
    take(rhs.at[0 : K - 32, 0:B], f_s)


def hand_on(tri, cross, tri_out, cross_out):
    tri_out[...] = tri[...]
    cross_out[...] = cross[...]


def local_step(am, bm, ap, bp):
    f32 = jnp.float32
    vmem = pltpu.VMEM
    dma = pltpu.SemaphoreType.DMA
    results = pl.pallas_call(
        kernel,
        out_shape=(jax.ShapeDtypeStruct((32, B), f32), jax.ShapeDtypeStruct((64, 256), f32)),
        in_specs=[pl.BlockSpec(memory_space=pl.ANY)] * 4,
        out_specs=[pl.BlockSpec(memory_space=pl.ANY)] * 2,
        scratch_shapes=[
            vmem((64, 256), f32),
            vmem((64, 256), f32),
            vmem((32, B), f32),
            vmem((COLS, B, B), f32),
            vmem((5, B, B), f32),
            vmem((5, ROWS, 8, B), f32),
            vmem((5, 8, B), f32),
            vmem((COLS, 8, B), f32),
            vmem((COLS, B, B), f32),
            vmem((K, K), f32),
            vmem((2, CHIPS, 32, 256), f32),
            vmem((2, CHIPS, 32, 256), f32),
            vmem((CHIPS, 32, 256), f32),
            vmem((CHIPS, 32, 256), f32),
            vmem((CHIPS, 32, 256), f32),
            vmem((CHIPS, 32, 256), f32),
            vmem((32, 256), f32),
            vmem((32, 256), f32),
            vmem((COLS, 32, 256), f32),
            vmem((K, 2 * B), f32),
            vmem((K, K), f32),
            vmem((COLS, B, B), f32),
            vmem((B, B), f32),
            vmem((B, B), f32),
            vmem((B, B), f32),
            dma, dma((COLS,)), dma,
            dma((5,)), dma((5,)),
            dma((5,)), dma((COLS,)), dma((COLS,)),
            dma((COLS,)), dma((COLS,)),
            dma((COLS,)), dma((COLS,)),
            dma((COLS,)), dma((COLS,)),
            dma((2,)), dma((2,)),
            dma, dma, dma, dma, dma, dma, dma, dma, dma, dma, dma, dma,
            dma((CHIPS,)), dma((4,)),
        ],
        compiler_params=pltpu.CompilerParams(
            collective_id=0, has_side_effects=True, vmem_limit_bytes=60 * 2**20
        ),
    )(am, bm, ap, bp)
    return pl.pallas_call(
        hand_on,
        out_shape=(jax.ShapeDtypeStruct((32, B), f32), jax.ShapeDtypeStruct((64, 256), f32)),
        in_specs=[pl.BlockSpec(memory_space=vmem)] * 2,
        out_specs=[pl.BlockSpec(memory_space=vmem)] * 2,
    )(*results)


def solution(mesh):
    spec = P("row", "col")
    return jax.shard_map(
        local_step, mesh=mesh, in_specs=(spec,) * 4, out_specs=(spec, spec), check_vma=False
    )
```
